32 devices in a mesh: cx: 2 (over x), cyz: 4 (over z), vert: 4 (over y, core).
Axes of the slice: x: 2, y: 2, z: 4, core: 2. Of those that a mesh axis runs over, the one named last changes fastest.
Arguments:
- dist: float32 [1728, 8, 32, 128], P('vert', 'cx', 'cyz'), may hold values from -40 to 40
- cell_type: int32 [8, 32, 128], P('cx', 'cyz'), may hold values from 0 to 3, as said below
- basis: float32 [13, 1728], P(None, 'vert'), may hold values from -0.15625 to 0.15625
- backmap: float32 [1728, 13], P('vert'), may hold values from -1.75 to 1.75
- source_map: float32 [13, 13], replicated, may hold values from -1.75 to 1.75
- coupling: float32 [13, 13], replicated, may hold values from -0.06 to 0.06
- diffusivity: float32 [13], replicated, may hold values from 0.5 to 8
- gradient_gain: float32 [13], replicated, may hold values from 0.1 to 1
Outputs:
- new_dist: bfloat16 [1728, 8, 32, 128], P('vert', 'cx', 'cyz')
- norms: float32 [5, 13], replicated
The draws below stay inside these ranges and needn't reach their ends.
Inputs may be any that keep to these rules, and one draw needn't show every extreme that they name: `cell_type`: 0 fluid, 1 wall, 2 inlet, 3 outlet; most cells are fluid.
All inputs are finite; a program needn't handle non-finite values.
Results may differ from the reference program's by a relative error of at most 0.001.
Values sent between devices are 32-bit elements; how exact they have to be, the bound alone decides.
A program may use at most 64 MiB of HBM per device.

```python
import math
import jax
import jax.numpy as jnp
from jax import lax

V = 1728
FIELDS = 13
ITERS = 4
NX = 8
NY = 32
NZ = 128


def draw_dist(key, part):
    base_key, rough_key = jax.random.split(key)
    full_shape = (V, NX, NY, NZ)
    base_draw = jnp.clip(jax.random.normal(base_key, full_shape, jnp.float32), -4.0, 4.0)
    rough_scale = jnp.exp(jax.random.uniform(rough_key, (1, NX, NY, NZ), jnp.float32, -1.15, 1.15))
    rising = 3.0 ** (jnp.arange(NY, dtype=jnp.float32) / NY)
    return base_draw * rough_scale * rising[None, None, :, None]


def draw_cell_type(key, part):
    ticket = jax.random.randint(key, (NX, NY, NZ), 0, 10)
    kinds = jnp.where(ticket < 7, 0, jnp.where(ticket < 8, 1, jnp.where(ticket < 9, 2, 3)))
    return kinds.astype(jnp.int32)


def block_scale(key, extent, cuts, least, top_value):
    loudness = 1.0
    for position, parts in cuts:
        heights = jax.random.uniform(jax.random.fold_in(jax.random.fold_in(key, 6), position), (parts,), jnp.float32, least / len(cuts), top_value / len(cuts))
        loudness = loudness * jnp.repeat(jnp.exp(heights), extent[position] // parts).reshape((-1,) + (1,) * (len(extent) - 1 - position))
    return loudness


def centred(stream_key, dims, spread, bound, shards=(), kind=jnp.bfloat16):
    array = spread * jax.random.normal(stream_key, dims, jnp.float32)
    if shards:
        array = array * block_scale(stream_key, dims, shards, -0.22, 0.18)
    return jnp.clip(array, -bound, bound).astype(kind)


def setup_inputs(seed: int = 0) -> dict:
    seeds = jax.random.split(jax.random.key(seed), 9)
    return {
        "dist": draw_dist(jax.random.fold_in(seeds[8], 71), 0),
        "cell_type": draw_cell_type(jax.random.fold_in(seeds[8], 71), 0),
        "basis": centred(seeds[2], (FIELDS, V), V ** -0.5, 0.15625, ((1, 4),), jnp.float32),
        "backmap": centred(seeds[3], (V, FIELDS), FIELDS ** -0.5, 1.75, ((0, 4),), jnp.float32),
        "source_map": centred(seeds[4], (FIELDS, FIELDS), FIELDS ** -0.5, 1.75, (), jnp.float32),
        "coupling": jnp.clip(jax.random.uniform(seeds[5], (FIELDS, FIELDS), jnp.float32, -0.06, 0.06), -0.06, 0.06),
        "diffusivity": jnp.clip(jnp.exp(jax.random.uniform(seeds[6], (FIELDS,), jnp.float32, math.log(0.5), math.log(8.0))), 0.5, 8.0),
        "gradient_gain": jnp.clip(jnp.exp(jax.random.uniform(seeds[7], (FIELDS,), jnp.float32, math.log(0.1), math.log(1.0))), 0.1, 1.0),
    }


highest = lax.Precision.HIGHEST

def laplace(field):
    padded = jnp.pad(field, ((0, 0), (1, 1), (1, 1), (1, 1)))
    near = padded[:, 2:, 1:-1, 1:-1] + padded[:, :-2, 1:-1, 1:-1]
    near = near + padded[:, 1:-1, 2:, 1:-1] + padded[:, 1:-1, :-2, 1:-1]
    near = near + padded[:, 1:-1, 1:-1, 2:] + padded[:, 1:-1, 1:-1, :-2]
    return 6.0 * field - near

def reference(dist, cell_type, basis, backmap, source_map, coupling, diffusivity, gradient_gain):
    moments = jnp.einsum('cv,vxyz->cxyz', basis, dist, precision=highest)
    fluid = (cell_type == 0).astype(jnp.float32)[None]
    inlet = (cell_type == 2).astype(jnp.float32)[None]
    outlet = (cell_type == 3).astype(jnp.float32)[None]
    active = fluid + outlet
    diffuse = diffusivity[:, None, None, None]
    mixed_source = jnp.einsum('cj,jxyz->cxyz', source_map, moments, precision=highest)
    target = active * (mixed_source - gradient_gain[:, None, None, None] * laplace(moments)) + inlet * moments
    diagonal = 1.0 + 6.0 * active * diffuse - fluid * jnp.diag(coupling)[:, None, None, None]

    def operate(field):
        coupled = jnp.einsum('cj,jxyz->cxyz', coupling, field, precision=highest)
        return field + active * diffuse * laplace(field) - fluid * coupled
    correction = jnp.zeros_like(target)
    resid = target
    squares = []
    for sweep in range(ITERS):
        squares.append(lax.optimization_barrier(jnp.sum(resid * resid, axis=(1, 2, 3))))
        omega = 1.0 / (1.0 + 0.8 * math.cos(math.pi * (2 * sweep + 1) / (2 * ITERS)))
        correction = correction + omega * resid / diagonal
        resid = target - operate(correction)
    squares.append(lax.optimization_barrier(jnp.sum(resid * resid, axis=(1, 2, 3))))
    norms = jnp.sqrt(jnp.stack(squares) / (NX * NY * NZ) + 1e-06)
    pieces = []
    for plane in range(NX):
        delta = jnp.einsum('vc,cyz->vyz', backmap, correction[:, plane], precision=highest)
        pieces.append((dist[:, plane] + delta).astype(jnp.bfloat16))
    new_dist = jnp.stack(pieces, axis=1)
    return (new_dist, norms)
```

```python
import functools
import math

import jax
import jax.numpy as jnp
from jax import lax
from jax.experimental import pallas as pl
from jax.experimental.pallas import tpu as pltpu
from jax.sharding import PartitionSpec as P

ITERS = 4
PAD = 16
CHUNKS = 3
MESH = pl.DeviceIdType.MESH
f32 = jnp.float32
bf16 = jnp.bfloat16


def halves(x):
    high = x.astype(bf16)
    return high, (x - high.astype(f32)).astype(bf16)


def kernel(
    sizes, dist, cell_type, basis, backmap, source_map, coupling, diffusivity, gain,
    out, norms,
    dist_v, out_v, delta_v, cells_v, basis_v, wide_v, back_v, backw_v, backs_v,
    part, arrived, field, xh, ystage, yh, planes_v, sq, first, second,
    dist_sem, small_sem, rs_s, rs_r, h_s, h_r, ag_s, ag_r, a1_s, a1_r, a2_s, a2_r, out_sem,
):
    ncx, ncyz, nv, fields, vel, rows, lanes = sizes
    cx, cyz, me = lax.axis_index("cx"), lax.axis_index("cyz"), lax.axis_index("vert")

    def at(c, y, v):
        return {"cx": c, "cyz": y, "vert": v}

    odd = cx % 2

    def plane_of(v):
        return v + odd * (nv - 1 - 2 * v)

    chip, core = me // 2, me % 2
    order = []
    for da in list(range(1, nv // 2)) + [0]:
        for db in (0, 1) if da else (1, 0):
            order.append(2 * ((chip + da) % (nv // 2)) + (core + db) % 2)
    last = nv - 1

    loads = []
    for step, owner in enumerate(order):
        copy = pltpu.make_async_copy(
            dist.at[:, plane_of(owner)], dist_v.at[step], dist_sem.at[step]
        )
        copy.start()
        loads.append(copy)
        if step == 0:
            get_basis = pltpu.make_async_copy(basis, basis_v, small_sem.at[0])
            get_basis.start()
    get_back = pltpu.make_async_copy(backmap, back_v, small_sem.at[1])
    get_cells = pltpu.make_async_copy(cell_type, cells_v, small_sem.at[2])
    get_back.start()
    get_cells.start()

    group = [
        (dx, dv) for dx in range(ncx) for dv in range(nv) if (dx, dv) != (0, 0)
    ]
    barrier = pltpu.get_barrier_semaphore()
    for dx, dv in group:
        pl.semaphore_signal(
            barrier, inc=1, device_id=at((cx + dx) % ncx, cyz, (me + dv) % nv), device_id_type=MESH
        )
    for dy in range(1, ncyz):
        pl.semaphore_signal(
            barrier, inc=1, device_id=at(cx, (cyz + dy) % ncyz, me), device_id_type=MESH
        )

    spot = plane_of(me)
    low, high = spot == 0, spot == nv - 1
    side = 1 - 2 * odd
    left = at(jnp.where(low, cx - 1, cx), cyz, jnp.where(low, me, me - side))
    right = at(jnp.where(high, cx + 1, cx), cyz, jnp.where(high, me, me + side))
    prev, following = at(cx, cyz - 1, me), at(cx, cyz + 1, me)
    place = cx * nv + spot
    has = [place > 0, place < ncx * nv - 1, cyz > 0, cyz < ncyz - 1]
    to = [left, right, prev, following]

    sq[...] = jnp.zeros_like(sq)
    planes_v[...] = jnp.zeros_like(planes_v)
    wide_v[...] = jnp.zeros_like(wide_v)
    for direction in range(2):

        @pl.when(jnp.logical_not(has[direction]))
        def _():
            for k in range(ITERS + 1):
                xh[k, direction] = jnp.zeros((fields * rows, lanes), f32)

        @pl.when(jnp.logical_not(has[2 + direction]))
        def _():
            for k in range(ITERS + 1):
                yh[k, direction] = jnp.zeros((fields, lanes), f32)

    get_basis.wait()
    wide_v[0:fields, :] = basis_v[...]
    weights = jnp.concatenate(halves(wide_v[...]), axis=0)

    def remote(src, dst, send, recv, device):
        return pltpu.make_async_remote_copy(
            src_ref=src, dst_ref=dst, send_sem=send, recv_sem=recv,
            device_id=device, device_id_type=MESH,
        )

    used = pl.ds(0, fields * rows)

    def scatter(owner, source):
        return remote(
            part.at[owner, used], arrived.at[source], rs_s.at[owner], rs_r.at[source],
            at(cx, cyz, owner),
        )

    for step, owner in enumerate(order):
        loads[step].wait()
        flat = dist_v.at[step].reshape(vel * rows, lanes)
        for y in range(0, rows, 2):
            pair = jnp.concatenate(
                [flat[pl.ds(y + i, vel, stride=rows), :] for i in range(2)], axis=1
            )
            top, rest = halves(pair)
            both = jnp.dot(weights, top, preferred_element_type=f32) + jnp.dot(
                weights, rest, preferred_element_type=f32
            )
            both = both[0:PAD] + both[PAD:]
            for i in range(2):
                part[owner, pl.ds(y + i, PAD, stride=rows), :] = both[:, i * lanes:(i + 1) * lanes]
        if step == 0:
            pl.semaphore_wait(barrier, len(group) + ncyz - 1)
        if step < last:
            scatter(owner, me).start()

    get_cells.wait()
    kinds = cells_v[spot]
    fluid = jnp.where(kinds == 0, 1.0, 0.0).astype(f32)
    inlet = jnp.where(kinds == 2, 1.0, 0.0).astype(f32)
    outlet = jnp.where(kinds == 3, 1.0, 0.0).astype(f32)
    active = fluid + outlet
    row = lax.broadcasted_iota(jnp.int32, (rows, lanes), 0)
    lane = lax.broadcasted_iota(jnp.int32, (rows, lanes), 1)

    def tile(c):
        return pl.ds(c * rows, rows)

    def mix(matrix, w):
        mixed = []
        for c in range(fields):
            total = matrix[c, 0] * w[0]
            for j in range(1, fields):
                total = total + matrix[c, j] * w[j]
            mixed.append(total)
        return mixed

    def halo(k, d):
        if d < 2:
            return remote(field.at[k], xh.at[k, 1 - d], h_s.at[k, d], h_r.at[k, 1 - d], to[d])
        return remote(
            ystage.at[k, d - 2], yh.at[k, 3 - d], h_s.at[k, d], h_r.at[k, 5 - d], to[d]
        )

    def landed(k, d):
        if d < 2:
            return remote(field.at[k], xh.at[k, d], h_s.at[k, d], h_r.at[k, d], to[d])
        return remote(ystage.at[k, d - 2], yh.at[k, d - 2], h_s.at[k, d], h_r.at[k, d], to[d])

    def start_halo(k, w):
        for c in range(fields):
            field[k, tile(c), :] = w[c]
            ystage[k, 0, pl.ds(c, 1), :] = w[c][0:1]
            ystage[k, 1, pl.ds(c, 1), :] = w[c][rows - 1:rows]
        for d in range(4):

            @pl.when(has[d])
            def _():
                halo(k, d).start()

    def wait_halo(k):
        for d in range(4):

            @pl.when(has[d])
            def _():
                landed(k, d).wait_recv()

    def laplace(k, w):
        result = []
        for c in range(fields):
            x = w[c]
            near = xh[k, 0, tile(c), :] + xh[k, 1, tile(c), :]
            above = jnp.broadcast_to(yh[k, 0, pl.ds(c, 1), :], (rows, lanes))
            below = jnp.broadcast_to(yh[k, 1, pl.ds(c, 1), :], (rows, lanes))
            near = near + jnp.where(row == 0, above, pltpu.roll(x, 1, 0))
            near = near + jnp.where(row == rows - 1, below, pltpu.roll(x, rows - 1, 0))
            near = near + jnp.where(lane == 0, 0.0, pltpu.roll(x, 1, 1))
            near = near + jnp.where(lane == lanes - 1, 0.0, pltpu.roll(x, lanes - 1, 1))
            result.append(6.0 * x - near)
        return result

    def keep_squares(k, r):
        for c in range(fields):
            sq[pl.ds(k * fields + c, 1), :] = jnp.sum(r[c] * r[c], axis=0, keepdims=True)

    for owner in order[:-1]:
        scatter(owner, owner).wait_recv()
    moments = []
    for c in range(fields):
        total = part[me, tile(c), :]
        for owner in order[:-1]:
            total = total + arrived[owner, tile(c), :]
        moments.append(total)

    start_halo(0, moments)
    mixed = mix(source_map, moments)
    inverse = [
        1.0 / (1.0 + 6.0 * active * diffusivity[c] - fluid * coupling[c, c])
        for c in range(fields)
    ]
    get_back.wait()
    backw_v[...] = jnp.zeros_like(backw_v)
    backw_v[:, 0:fields] = back_v[...]
    wide = backw_v[...]
    top = wide.astype(bf16).astype(f32)
    rest = wide - top
    backs_v[...] = (
        top + pltpu.roll(top, PAD, 1) + pltpu.roll(rest, 2 * PAD, 1) + pltpu.roll(rest, 3 * PAD, 1)
    ).astype(bf16)
    wait_halo(0)
    bent = laplace(0, moments)
    target = [
        active * (mixed[c] - gain[c] * bent[c]) + inlet * moments[c] for c in range(fields)
    ]

    def omega(k):
        return 1.0 / (1.0 + 0.8 * math.cos(math.pi * (2 * k + 1) / (2 * ITERS)))

    def residual(k, w, coupled):
        bent = laplace(k, w)
        return [
            target[c] - (w[c] + active * diffusivity[c] * bent[c] - fluid * coupled[c])
            for c in range(fields)
        ]

    correction = [omega(0) * target[c] * inverse[c] for c in range(fields)]
    resid = target
    for k in range(1, ITERS):
        start_halo(k, correction)
        keep_squares(k - 1, resid)
        coupled = mix(coupling, correction)
        wait_halo(k)
        resid = residual(k, correction, coupled)
        correction = [
            correction[c] + omega(k) * resid[c] * inverse[c] for c in range(fields)
        ]
    start_halo(ITERS, correction)
    for c in range(fields):
        planes_v[me, tile(c), :] = correction[c]

    def gather(source, peer):
        return remote(
            planes_v.at[source, used], planes_v.at[source, used], ag_s.at[peer], ag_r.at[source],
            at(cx, cyz, peer),
        )

    for owner in order[:-1]:
        gather(me, owner).start()
    keep_squares(ITERS - 1, resid)
    coupled = mix(coupling, correction)

    size = vel // CHUNKS
    stores = []

    def finish(step):
        owner = order[step]
        if step < last:
            gather(owner, owner).wait_recv()
        columns = jnp.concatenate(
            [planes_v[owner, pl.ds(y, PAD, stride=rows), :] for y in range(rows)], axis=1
        )
        top, rest = halves(columns)
        stacked = jnp.concatenate(
            [top, rest, top, rest, jnp.zeros((lanes - 4 * PAD, rows * lanes), bf16)], axis=0
        )
        for chunk in range(CHUNKS):
            span = pl.ds(chunk * size, size)
            flat = delta_v.at[chunk].reshape(size * rows, lanes)
            for y in range(0, rows, 2):
                delta = jnp.dot(
                    backs_v[span, :], stacked[:, y * lanes:(y + 2) * lanes],
                    preferred_element_type=f32,
                )
                for i in range(2):
                    flat[pl.ds(y + i, size, stride=rows), :] = delta[:, i * lanes:(i + 1) * lanes]
            out_v[step, span] = (dist_v[step, span] + delta_v[chunk]).astype(bf16)
        copy = pltpu.make_async_copy(out_v.at[step], out.at[:, plane_of(owner)], out_sem.at[step])
        copy.start()
        stores.append(copy)

    finish(last)
    wait_halo(ITERS)
    keep_squares(ITERS, residual(ITERS, correction, coupled))
    mine = cx * nv + me
    first[mine] = lax.dot_general(
        jnp.ones((rows, lanes), f32), sq[...], (((1,), (1,)), ((), ())),
        precision=lax.Precision.HIGHEST, preferred_element_type=f32,
    )

    def sum_first(slot, index, c, v):
        return remote(first.at[slot], first.at[slot], a1_s.at[index], a1_r.at[slot], at(c, cyz, v))

    def sum_second(slot, index, y):
        return remote(second.at[slot], second.at[slot], a2_s.at[index], a2_r.at[slot], at(cx, y, me))

    for index, (dx, dv) in enumerate(group):
        sum_first(mine, index, (cx + dx) % ncx, (me + dv) % nv).start()
    finish(last - 1)
    for index, (dx, dv) in enumerate(group):
        c, v = (cx + dx) % ncx, (me + dv) % nv
        sum_first(c * nv + v, index, c, v).wait_recv()
    total = first[0]
    for i in range(1, ncx * nv):
        total = total + first[i]
    second[cyz] = total
    for dy in range(1, ncyz):
        sum_second(cyz, dy, (cyz + dy) % ncyz).start()
    for step in range(last - 2, -1, -1):
        finish(step)
    for dy in range(1, ncyz):
        y = (cyz + dy) % ncyz
        sum_second(y, dy, y).wait_recv()
    total = second[0]
    for i in range(1, ncyz):
        total = total + second[i]
    value = jnp.sqrt(total / (ncx * nv * rows * ncyz * lanes) + 1e-06)
    for k in range(ITERS + 1):
        shifted = value if k == 0 else pltpu.roll(value, lanes - k * fields, 1)
        norms[pl.ds(k, 1), :] = shifted[0:1, 0:fields]

    for owner in order[:-1]:
        scatter(owner, me).wait_send()
        gather(me, owner).wait_send()
    for k in range(ITERS + 1):
        for d in range(4):

            @pl.when(has[d])
            def _():
                halo(k, d).wait_send()

    for index, (dx, dv) in enumerate(group):
        sum_first(mine, index, (cx + dx) % ncx, (me + dv) % nv).wait_send()
    for dy in range(1, ncyz):
        sum_second(cyz, dy, (cyz + dy) % ncyz).wait_send()
    for copy in stores:
        copy.wait()


def local(mesh_shape, *args):
    dist, cell_type, basis = args[:3]
    ncx, ncyz, nv = mesh_shape
    vel, planes, rows, lanes = dist.shape
    fields = basis.shape[0]
    assert planes == nv and nv % 2 == 0 and vel % (CHUNKS * 16) == 0
    sizes = (ncx, ncyz, nv, fields, vel, rows, lanes)
    anywhere = pl.BlockSpec(memory_space=pl.ANY)
    scalars = pl.BlockSpec(memory_space=pltpu.SMEM)
    rounds = ITERS + 1
    dma = pltpu.SemaphoreType.DMA
    deep = fields * rows
    return pl.pallas_call(
        functools.partial(kernel, sizes),
        out_shape=(
            jax.ShapeDtypeStruct(dist.shape, bf16),
            jax.ShapeDtypeStruct((rounds, fields), f32),
        ),
        in_specs=[anywhere] * 4 + [scalars] * 4,
        out_specs=(anywhere, pl.BlockSpec(memory_space=pltpu.VMEM)),
        scratch_shapes=[
            pltpu.VMEM((nv, vel, rows, lanes), f32),
            pltpu.VMEM((nv, vel, rows, lanes), bf16),
            pltpu.VMEM((CHUNKS, vel // CHUNKS, rows, lanes), f32),
            pltpu.VMEM(cell_type.shape, jnp.int32),
            pltpu.VMEM((fields, vel), f32),
            pltpu.VMEM((PAD, vel), f32),
            pltpu.VMEM((vel, fields), f32),
            pltpu.VMEM((vel, lanes), f32),
            pltpu.VMEM((vel, lanes), bf16),
            pltpu.VMEM((nv, PAD * rows, lanes), f32),
            pltpu.VMEM((nv, deep, lanes), f32),
            pltpu.VMEM((rounds, deep, lanes), f32),
            pltpu.VMEM((rounds, 2, deep, lanes), f32),
            pltpu.VMEM((rounds, 2, fields, lanes), f32),
            pltpu.VMEM((rounds, 2, fields, lanes), f32),
            pltpu.VMEM((nv, PAD * rows, lanes), f32),
            pltpu.VMEM((lanes, lanes), f32),
            pltpu.VMEM((ncx * nv, rows, lanes), f32),
            pltpu.VMEM((ncyz, rows, lanes), f32),
            dma((nv,)), dma((3,)), dma((nv,)), dma((nv,)),
            dma((rounds, 4)), dma((rounds, 4)), dma((nv,)), dma((nv,)),
            dma((ncx * nv,)), dma((ncx * nv,)), dma((ncyz,)), dma((ncyz,)), dma((nv,)),
        ],
        compiler_params=pltpu.CompilerParams(
            collective_id=0, has_side_effects=True, vmem_limit_bytes=40 * 2**20
        ),
    )(*args)


def solution(mesh):
    placed = (
        P("vert", "cx", "cyz", None),
        P("cx", "cyz", None),
        P(None, "vert"),
        P("vert", None),
        P(),
        P(),
        P(),
        P(),
    )
    shape = tuple(mesh.shape[name] for name in ("cx", "cyz", "vert"))
    return jax.shard_map(
        functools.partial(local, shape),
        mesh=mesh,
        in_specs=placed,
        out_specs=(P("vert", "cx", "cyz", None), P()),
        check_vma=False,
    )
```

```python
import functools
import math

import jax
import jax.numpy as jnp
from jax import lax
from jax.experimental import pallas as pl
from jax.experimental.pallas import tpu as pltpu
from jax.sharding import PartitionSpec as P

ITERS = 4
PAD = 16
CHUNKS = 3
MESH = pl.DeviceIdType.MESH
f32 = jnp.float32
bf16 = jnp.bfloat16


def halves(x):
    high = x.astype(bf16)
    return high, (x - high.astype(f32)).astype(bf16)


def kernel(
    sizes, dist, cell_type, basis, backmap, source_map, coupling, diffusivity, gain,
    out, norms,
    dist_v, out_v, delta_v, cells_v, basis_v, wide_v, back_v, backw_v, backs_v,
    part, arrived, field, xh, ystage, yh, planes_v, sq, first, second,
    dist_sem, small_sem, rs_s, rs_r, h_s, h_r, ag_s, ag_r, a1_s, a1_r, a2_s, a2_r, out_sem,
):
    ncx, ncyz, nv, fields, vel, rows, lanes = sizes
    cx, cyz, me = lax.axis_index("cx"), lax.axis_index("cyz"), lax.axis_index("vert")

    def at(c, y, v):
        return {"cx": c, "cyz": y, "vert": v}

    odd = cx % 2

    def plane_of(v):
        return v + odd * (nv - 1 - 2 * v)

    chip, core = me // 2, me % 2
    order = []
    for da in list(range(1, nv // 2)) + [0]:
        for db in (0, 1) if da else (1, 0):
            order.append(2 * ((chip + da) % (nv // 2)) + (core + db) % 2)
    last = nv - 1

    loads = []
    for step, owner in enumerate(order):
        copy = pltpu.make_async_copy(
            dist.at[:, plane_of(owner)], dist_v.at[step], dist_sem.at[step]
        )
        copy.start()
        loads.append(copy)
        if step == 0:
            get_basis = pltpu.make_async_copy(basis, basis_v, small_sem.at[0])
            get_basis.start()
    get_back = pltpu.make_async_copy(backmap, back_v, small_sem.at[1])
    get_cells = pltpu.make_async_copy(cell_type, cells_v, small_sem.at[2])
    get_back.start()
    get_cells.start()

    group = [
        (dx, dv) for dx in range(ncx) for dv in range(nv) if (dx, dv) != (0, 0)
    ]
    barrier = pltpu.get_barrier_semaphore()
    for dx, dv in group:
        pl.semaphore_signal(
            barrier, inc=1, device_id=at((cx + dx) % ncx, cyz, (me + dv) % nv), device_id_type=MESH
        )
    for dy in range(1, ncyz):
        pl.semaphore_signal(
            barrier, inc=1, device_id=at(cx, (cyz + dy) % ncyz, me), device_id_type=MESH
        )

    spot = plane_of(me)
    low, high = spot == 0, spot == nv - 1
    side = 1 - 2 * odd
    left = at(jnp.where(low, cx - 1, cx), cyz, jnp.where(low, me, me - side))
    right = at(jnp.where(high, cx + 1, cx), cyz, jnp.where(high, me, me + side))
    prev, following = at(cx, cyz - 1, me), at(cx, cyz + 1, me)
    place = cx * nv + spot
    has = [place > 0, place < ncx * nv - 1, cyz > 0, cyz < ncyz - 1]
    to = [left, right, prev, following]

    sq[...] = jnp.zeros_like(sq)
    planes_v[...] = jnp.zeros_like(planes_v)
    wide_v[...] = jnp.zeros_like(wide_v)
    for direction in range(2):

        @pl.when(jnp.logical_not(has[direction]))
        def _():
            for k in range(ITERS + 1):
                xh[k, direction] = jnp.zeros((fields * rows, lanes), f32)

        @pl.when(jnp.logical_not(has[2 + direction]))
        def _():
            for k in range(ITERS + 1):
                yh[k, direction] = jnp.zeros((fields, lanes), f32)

    get_basis.wait()
    wide_v[0:fields, :] = basis_v[...]
    weights = jnp.concatenate(halves(wide_v[...]), axis=0)

    def remote(src, dst, send, recv, device):
        return pltpu.make_async_remote_copy(
            src_ref=src, dst_ref=dst, send_sem=send, recv_sem=recv,
            device_id=device, device_id_type=MESH,
        )

    used = pl.ds(0, fields * rows)

    def scatter(owner, source):
        return remote(
            part.at[owner, used], arrived.at[source], rs_s.at[owner], rs_r.at[source],
            at(cx, cyz, owner),
        )

    for step, owner in enumerate(order):
        loads[step].wait()
        flat = dist_v.at[step].reshape(vel * rows, lanes)
        for y in range(0, rows, 2):
            pair = jnp.concatenate(
                [flat[pl.ds(y + i, vel, stride=rows), :] for i in range(2)], axis=1
            )
            top, rest = halves(pair)
            both = jnp.dot(weights, top, preferred_element_type=f32) + jnp.dot(
                weights, rest, preferred_element_type=f32
            )
            both = both[0:PAD] + both[PAD:]
            for i in range(2):
                part[owner, pl.ds(y + i, PAD, stride=rows), :] = both[:, i * lanes:(i + 1) * lanes]
        if step == 0:
            pl.semaphore_wait(barrier, len(group) + ncyz - 1)
        if step < last:
            scatter(owner, me).start()

    get_cells.wait()
    kinds = cells_v[spot]
    fluid = jnp.where(kinds == 0, 1.0, 0.0).astype(f32)
    inlet = jnp.where(kinds == 2, 1.0, 0.0).astype(f32)
    outlet = jnp.where(kinds == 3, 1.0, 0.0).astype(f32)
    active = fluid + outlet
    row = lax.broadcasted_iota(jnp.int32, (rows, lanes), 0)
    lane = lax.broadcasted_iota(jnp.int32, (rows, lanes), 1)

    def tile(c):
        return pl.ds(c * rows, rows)

    def mix(matrix, w):
        mixed = []
        for c in range(fields):
            total = matrix[c, 0] * w[0]
            for j in range(1, fields):
                total = total + matrix[c, j] * w[j]
            mixed.append(total)
        return mixed

    def halo(k, d):
        if d < 2:
            return remote(field.at[k], xh.at[k, 1 - d], h_s.at[k, d], h_r.at[k, 1 - d], to[d])
        return remote(
            ystage.at[k, d - 2], yh.at[k, 3 - d], h_s.at[k, d], h_r.at[k, 5 - d], to[d]
        )

    def landed(k, d):
        if d < 2:
            return remote(field.at[k], xh.at[k, d], h_s.at[k, d], h_r.at[k, d], to[d])
        return remote(ystage.at[k, d - 2], yh.at[k, d - 2], h_s.at[k, d], h_r.at[k, d], to[d])

    def start_halo(k, w):
        for c in range(fields):
            field[k, tile(c), :] = w[c]
            ystage[k, 0, pl.ds(c, 1), :] = w[c][0:1]
            ystage[k, 1, pl.ds(c, 1), :] = w[c][rows - 1:rows]
        for d in range(4):

            @pl.when(has[d])
            def _():
                halo(k, d).start()

    def wait_halo(k):
        for d in range(4):

            @pl.when(has[d])
            def _():
                landed(k, d).wait_recv()

    def laplace(k, w):
        result = []
        for c in range(fields):
            x = w[c]
            near = xh[k, 0, tile(c), :] + xh[k, 1, tile(c), :]
            above = jnp.broadcast_to(yh[k, 0, pl.ds(c, 1), :], (rows, lanes))
            below = jnp.broadcast_to(yh[k, 1, pl.ds(c, 1), :], (rows, lanes))
            near = near + jnp.where(row == 0, above, pltpu.roll(x, 1, 0))
            near = near + jnp.where(row == rows - 1, below, pltpu.roll(x, rows - 1, 0))
            near = near + jnp.where(lane == 0, 0.0, pltpu.roll(x, 1, 1))
            near = near + jnp.where(lane == lanes - 1, 0.0, pltpu.roll(x, lanes - 1, 1))
            result.append(6.0 * x - near)
        return result

    def keep_squares(k, r):
        for c in range(fields):
            sq[pl.ds(k * fields + c, 1), :] = jnp.sum(r[c] * r[c], axis=0, keepdims=True)

    for owner in order[:-1]:
        scatter(owner, owner).wait_recv()
    moments = []
    for c in range(fields):
        total = part[me, tile(c), :]
        for owner in order[:-1]:
            total = total + arrived[owner, tile(c), :]
        moments.append(total)

    start_halo(0, moments)
    mixed = mix(source_map, moments)
    inverse = [
        1.0 / (1.0 + 6.0 * active * diffusivity[c] - fluid * coupling[c, c])
        for c in range(fields)
    ]
    get_back.wait()
    backw_v[...] = jnp.zeros_like(backw_v)
    backw_v[0:fields, 0:vel] = back_v[...]
    wide = backw_v[...]
    top = wide.astype(bf16).astype(f32)
    rest = wide - top
    turned = jnp.concatenate(
        [top, top, rest, rest, jnp.zeros((lanes - 4 * PAD, wide.shape[1]), f32)], axis=0
    ).T
    backs_v[...] = turned[0:vel].astype(bf16)
    wait_halo(0)
    bent = laplace(0, moments)
    target = [
        active * (mixed[c] - gain[c] * bent[c]) + inlet * moments[c] for c in range(fields)
    ]

    def omega(k):
        return 1.0 / (1.0 + 0.8 * math.cos(math.pi * (2 * k + 1) / (2 * ITERS)))

    def residual(k, w, coupled):
        bent = laplace(k, w)
        return [
            target[c] - (w[c] + active * diffusivity[c] * bent[c] - fluid * coupled[c])
            for c in range(fields)
        ]

    correction = [omega(0) * target[c] * inverse[c] for c in range(fields)]
    resid = target
    for k in range(1, ITERS):
        start_halo(k, correction)
        keep_squares(k - 1, resid)
        coupled = mix(coupling, correction)
        wait_halo(k)
        resid = residual(k, correction, coupled)
        correction = [
            correction[c] + omega(k) * resid[c] * inverse[c] for c in range(fields)
        ]
    start_halo(ITERS, correction)
    for c in range(fields):
        planes_v[me, tile(c), :] = correction[c]

    def gather(source, peer):
        return remote(
            planes_v.at[source, used], planes_v.at[source, used], ag_s.at[peer], ag_r.at[source],
            at(cx, cyz, peer),
        )

    for owner in order[:-1]:
        gather(me, owner).start()
    keep_squares(ITERS - 1, resid)
    coupled = mix(coupling, correction)

    size = vel // CHUNKS
    stores = []

    def finish(step):
        owner = order[step]
        if step < last:
            gather(owner, owner).wait_recv()
        columns = jnp.concatenate(
            [planes_v[owner, pl.ds(y, PAD, stride=rows), :] for y in range(rows)], axis=1
        )
        top, rest = halves(columns)
        stacked = jnp.concatenate(
            [top, rest, top, rest, jnp.zeros((lanes - 4 * PAD, rows * lanes), bf16)], axis=0
        )
        for chunk in range(CHUNKS):
            span = pl.ds(chunk * size, size)
            flat = delta_v.at[chunk].reshape(size * rows, lanes)
            for y in range(0, rows, 2):
                delta = jnp.dot(
                    backs_v[span, :], stacked[:, y * lanes:(y + 2) * lanes],
                    preferred_element_type=f32,
                )
                for i in range(2):
                    flat[pl.ds(y + i, size, stride=rows), :] = delta[:, i * lanes:(i + 1) * lanes]
            out_v[step, span] = (dist_v[step, span] + delta_v[chunk]).astype(bf16)
        copy = pltpu.make_async_copy(out_v.at[step], out.at[:, plane_of(owner)], out_sem.at[step])
        copy.start()
        stores.append(copy)

    finish(last)
    wait_halo(ITERS)
    keep_squares(ITERS, residual(ITERS, correction, coupled))
    mine = cx * nv + me
    first[mine] = lax.dot_general(
        jnp.ones((rows, lanes), f32), sq[...], (((1,), (1,)), ((), ())),
        precision=lax.Precision.HIGHEST, preferred_element_type=f32,
    )

    def sum_first(slot, index, c, v):
        return remote(first.at[slot], first.at[slot], a1_s.at[index], a1_r.at[slot], at(c, cyz, v))

    def sum_second(slot, index, y):
        return remote(second.at[slot], second.at[slot], a2_s.at[index], a2_r.at[slot], at(cx, y, me))

    for index, (dx, dv) in enumerate(group):
        sum_first(mine, index, (cx + dx) % ncx, (me + dv) % nv).start()
    finish(last - 1)
    for index, (dx, dv) in enumerate(group):
        c, v = (cx + dx) % ncx, (me + dv) % nv
        sum_first(c * nv + v, index, c, v).wait_recv()
    total = first[0]
    for i in range(1, ncx * nv):
        total = total + first[i]
    second[cyz] = total
    for dy in range(1, ncyz):
        sum_second(cyz, dy, (cyz + dy) % ncyz).start()
    for step in range(last - 2, -1, -1):
        finish(step)
    for dy in range(1, ncyz):
        y = (cyz + dy) % ncyz
        sum_second(y, dy, y).wait_recv()
    total = second[0]
    for i in range(1, ncyz):
        total = total + second[i]
    value = jnp.sqrt(total / (ncx * nv * rows * ncyz * lanes) + 1e-06)
    for k in range(ITERS + 1):
        shifted = value if k == 0 else pltpu.roll(value, lanes - k * fields, 1)
        norms[pl.ds(k, 1), :] = shifted[0:1, 0:fields]

    for owner in order[:-1]:
        scatter(owner, me).wait_send()
        gather(me, owner).wait_send()
    for k in range(ITERS + 1):
        for d in range(4):

            @pl.when(has[d])
            def _():
                halo(k, d).wait_send()

    for index, (dx, dv) in enumerate(group):
        sum_first(mine, index, (cx + dx) % ncx, (me + dv) % nv).wait_send()
    for dy in range(1, ncyz):
        sum_second(cyz, dy, (cyz + dy) % ncyz).wait_send()
    for copy in stores:
        copy.wait()


def local(mesh_shape, *args):
    dist, cell_type, basis = args[:3]
    ncx, ncyz, nv = mesh_shape
    vel, planes, rows, lanes = dist.shape
    fields = basis.shape[0]
    assert planes == nv and nv % 2 == 0 and vel % (CHUNKS * 16) == 0
    sizes = (ncx, ncyz, nv, fields, vel, rows, lanes)
    anywhere = pl.BlockSpec(memory_space=pl.ANY)
    scalars = pl.BlockSpec(memory_space=pltpu.SMEM)
    rounds = ITERS + 1
    dma = pltpu.SemaphoreType.DMA
    deep = fields * rows
    return pl.pallas_call(
        functools.partial(kernel, sizes),
        out_shape=(
            jax.ShapeDtypeStruct(dist.shape, bf16),
            jax.ShapeDtypeStruct((rounds, fields), f32),
        ),
        in_specs=[anywhere] * 4 + [scalars] * 4,
        out_specs=(anywhere, pl.BlockSpec(memory_space=pltpu.VMEM)),
        scratch_shapes=[
            pltpu.VMEM((nv, vel, rows, lanes), f32),
            pltpu.VMEM((nv, vel, rows, lanes), bf16),
            pltpu.VMEM((CHUNKS, vel // CHUNKS, rows, lanes), f32),
            pltpu.VMEM(cell_type.shape, jnp.int32),
            pltpu.VMEM((fields, vel), f32),
            pltpu.VMEM((PAD, vel), f32),
            pltpu.VMEM((fields, vel), f32),
            pltpu.VMEM((PAD, -(-vel // lanes) * lanes), f32),
            pltpu.VMEM((vel, lanes), bf16),
            pltpu.VMEM((nv, PAD * rows, lanes), f32),
            pltpu.VMEM((nv, deep, lanes), f32),
            pltpu.VMEM((rounds, deep, lanes), f32),
            pltpu.VMEM((rounds, 2, deep, lanes), f32),
            pltpu.VMEM((rounds, 2, fields, lanes), f32),
            pltpu.VMEM((rounds, 2, fields, lanes), f32),
            pltpu.VMEM((nv, PAD * rows, lanes), f32),
            pltpu.VMEM((lanes, lanes), f32),
            pltpu.VMEM((ncx * nv, rows, lanes), f32),
            pltpu.VMEM((ncyz, rows, lanes), f32),
            dma((nv,)), dma((3,)), dma((nv,)), dma((nv,)),
            dma((rounds, 4)), dma((rounds, 4)), dma((nv,)), dma((nv,)),
            dma((ncx * nv,)), dma((ncx * nv,)), dma((ncyz,)), dma((ncyz,)), dma((nv,)),
        ],
        compiler_params=pltpu.CompilerParams(
            collective_id=0, has_side_effects=True, vmem_limit_bytes=67043328
        ),
    )(*args[:3], args[3].T, *args[4:])


def solution(mesh):
    placed = (
        P("vert", "cx", "cyz", None),
        P("cx", "cyz", None),
        P(None, "vert"),
        P("vert", None),
        P(),
        P(),
        P(),
        P(),
    )
    shape = tuple(mesh.shape[name] for name in ("cx", "cyz", "vert"))
    return jax.shard_map(
        functools.partial(local, shape),
        mesh=mesh,
        in_specs=placed,
        out_specs=(P("vert", "cx", "cyz", None), P()),
        check_vma=False,
    )
```

```python
import functools
import math

import jax
import jax.numpy as jnp
from jax import lax
from jax.experimental import pallas as pl
from jax.experimental.pallas import tpu as pltpu
from jax.sharding import PartitionSpec as P

ITERS = 4
PAD = 16
CHUNKS = 3
MESH = pl.DeviceIdType.MESH
f32 = jnp.float32
bf16 = jnp.bfloat16


def halves(x):
    high = x.astype(bf16)
    return high, (x - high.astype(f32)).astype(bf16)


def kernel(
    sizes, dist, cell_type, basis, backmap, source_hbm, coupling_hbm, diffusivity_hbm, gain_hbm,
    out, norms,
    source_map, coupling, diffusivity, gain, dist_v, out_v, delta_v, cells_v, basis_v, wide_v, back_v, backw_v, backs_v,
    part, arrived, field, xh, ystage, yh, planes_v, sq, first, second,
    dist_sem, small_sem, rs_s, rs_r, h_s, h_r, ag_s, ag_r, a1_s, a1_r, a2_s, a2_r, out_sem,
):
    ncx, ncyz, nv, fields, vel, rows, lanes = sizes
    cx, cyz, me = lax.axis_index("cx"), lax.axis_index("cyz"), lax.axis_index("vert")

    def at(c, y, v):
        return {"cx": c, "cyz": y, "vert": v}

    odd = cx % 2

    def plane_of(v):
        return v + odd * (nv - 1 - 2 * v)

    chip, core = me // 2, me % 2
    order = []
    for da in list(range(1, nv // 2)) + [0]:
        for db in (0, 1) if da else (1, 0):
            order.append(2 * ((chip + da) % (nv // 2)) + (core + db) % 2)
    last = nv - 1

    loads = []
    for step, owner in enumerate(order):
        copy = pltpu.make_async_copy(
            dist.at[:, plane_of(owner)], dist_v.at[step], dist_sem.at[step]
        )
        copy.start()
        loads.append(copy)
        if step == 0:
            get_basis = pltpu.make_async_copy(basis, basis_v, small_sem.at[0])
            get_basis.start()
    get_back = pltpu.make_async_copy(backmap, back_v, small_sem.at[1])
    get_cells = pltpu.make_async_copy(cell_type, cells_v, small_sem.at[2])
    get_back.start()
    get_cells.start()
    scalars = [
        pltpu.make_async_copy(a, b, small_sem.at[3 + i])
        for i, (a, b) in enumerate((
            (source_hbm, source_map), (coupling_hbm, coupling),
            (diffusivity_hbm, diffusivity), (gain_hbm, gain),
        ))
    ]
    for copy in scalars:
        copy.start()

    group = [
        (dx, dv) for dx in range(ncx) for dv in range(nv) if (dx, dv) != (0, 0)
    ]
    barrier = pltpu.get_barrier_semaphore()
    for dx, dv in group:
        pl.semaphore_signal(
            barrier, inc=1, device_id=at((cx + dx) % ncx, cyz, (me + dv) % nv), device_id_type=MESH
        )
    for dy in range(1, ncyz):
        pl.semaphore_signal(
            barrier, inc=1, device_id=at(cx, (cyz + dy) % ncyz, me), device_id_type=MESH
        )

    spot = plane_of(me)
    low, high = spot == 0, spot == nv - 1
    side = 1 - 2 * odd
    left = at(jnp.where(low, cx - 1, cx), cyz, jnp.where(low, me, me - side))
    right = at(jnp.where(high, cx + 1, cx), cyz, jnp.where(high, me, me + side))
    prev, following = at(cx, cyz - 1, me), at(cx, cyz + 1, me)
    place = cx * nv + spot
    has = [place > 0, place < ncx * nv - 1, cyz > 0, cyz < ncyz - 1]
    to = [left, right, prev, following]

    sq[...] = jnp.zeros_like(sq)
    planes_v[...] = jnp.zeros_like(planes_v)
    wide_v[...] = jnp.zeros_like(wide_v)
    for direction in range(2):

        @pl.when(jnp.logical_not(has[direction]))
        def _():
            for k in range(ITERS + 1):
                xh[k, direction] = jnp.zeros((fields * rows, lanes), f32)

        @pl.when(jnp.logical_not(has[2 + direction]))
        def _():
            for k in range(ITERS + 1):
                yh[k, direction] = jnp.zeros((fields, lanes), f32)

    get_basis.wait()
    wide_v[0:fields, :] = basis_v[...]
    weights = jnp.concatenate(halves(wide_v[...]), axis=0)

    def remote(src, dst, send, recv, device):
        return pltpu.make_async_remote_copy(
            src_ref=src, dst_ref=dst, send_sem=send, recv_sem=recv,
            device_id=device, device_id_type=MESH,
        )

    used = pl.ds(0, fields * rows)

    def scatter(owner, source):
        return remote(
            part.at[owner, used], arrived.at[source], rs_s.at[owner], rs_r.at[source],
            at(cx, cyz, owner),
        )

    for step, owner in enumerate(order):
        loads[step].wait()
        flat = dist_v.at[step].reshape(vel * rows, lanes)
        for y in range(0, rows, 2):
            pair = jnp.concatenate(
                [flat[pl.ds(y + i, vel, stride=rows), :] for i in range(2)], axis=1
            )
            top, rest = halves(pair)
            both = jnp.dot(weights, top, preferred_element_type=f32) + jnp.dot(
                weights, rest, preferred_element_type=f32
            )
            both = both[0:PAD] + both[PAD:]
            for i in range(2):
                part[owner, pl.ds(y + i, PAD, stride=rows), :] = both[:, i * lanes:(i + 1) * lanes]
        if step == 0:
            pl.semaphore_wait(barrier, len(group) + ncyz - 1)
        if step < last:
            scatter(owner, me).start()

    get_cells.wait()
    for copy in scalars:
        copy.wait()
    kinds = cells_v[spot]
    fluid = jnp.where(kinds == 0, 1.0, 0.0).astype(f32)
    inlet = jnp.where(kinds == 2, 1.0, 0.0).astype(f32)
    outlet = jnp.where(kinds == 3, 1.0, 0.0).astype(f32)
    active = fluid + outlet
    row = lax.broadcasted_iota(jnp.int32, (rows, lanes), 0)
    lane = lax.broadcasted_iota(jnp.int32, (rows, lanes), 1)

    def tile(c):
        return pl.ds(c * rows, rows)

    def mix(matrix, w):
        mixed = []
        for c in range(fields):
            total = matrix[c, 0] * w[0]
            for j in range(1, fields):
                total = total + matrix[c, j] * w[j]
            mixed.append(total)
        return mixed

    def halo(k, d):
        if d < 2:
            return remote(field.at[k], xh.at[k, 1 - d], h_s.at[k, d], h_r.at[k, 1 - d], to[d])
        return remote(
            ystage.at[k, d - 2], yh.at[k, 3 - d], h_s.at[k, d], h_r.at[k, 5 - d], to[d]
        )

    def landed(k, d):
        if d < 2:
            return remote(field.at[k], xh.at[k, d], h_s.at[k, d], h_r.at[k, d], to[d])
        return remote(ystage.at[k, d - 2], yh.at[k, d - 2], h_s.at[k, d], h_r.at[k, d], to[d])

    def start_halo(k, w):
        for c in range(fields):
            field[k, tile(c), :] = w[c]
            ystage[k, 0, pl.ds(c, 1), :] = w[c][0:1]
            ystage[k, 1, pl.ds(c, 1), :] = w[c][rows - 1:rows]
        for d in range(4):

            @pl.when(has[d])
            def _():
                halo(k, d).start()

    def wait_halo(k):
        for d in range(4):

            @pl.when(has[d])
            def _():
                landed(k, d).wait_recv()

    def laplace(k, w):
        result = []
        for c in range(fields):
            x = w[c]
            near = xh[k, 0, tile(c), :] + xh[k, 1, tile(c), :]
            above = jnp.broadcast_to(yh[k, 0, pl.ds(c, 1), :], (rows, lanes))
            below = jnp.broadcast_to(yh[k, 1, pl.ds(c, 1), :], (rows, lanes))
            near = near + jnp.where(row == 0, above, pltpu.roll(x, 1, 0))
            near = near + jnp.where(row == rows - 1, below, pltpu.roll(x, rows - 1, 0))
            near = near + jnp.where(lane == 0, 0.0, pltpu.roll(x, 1, 1))
            near = near + jnp.where(lane == lanes - 1, 0.0, pltpu.roll(x, lanes - 1, 1))
            result.append(6.0 * x - near)
        return result

    def keep_squares(k, r):
        for c in range(fields):
            sq[pl.ds(k * fields + c, 1), :] = jnp.sum(r[c] * r[c], axis=0, keepdims=True)

    for owner in order[:-1]:
        scatter(owner, owner).wait_recv()
    moments = []
    for c in range(fields):
        total = part[me, tile(c), :]
        for owner in order[:-1]:
            total = total + arrived[owner, tile(c), :]
        moments.append(total)

    start_halo(0, moments)
    mixed = mix(source_map, moments)
    inverse = [
        1.0 / (1.0 + 6.0 * active * diffusivity[c] - fluid * coupling[c, c])
        for c in range(fields)
    ]
    get_back.wait()
    backw_v[...] = jnp.zeros_like(backw_v)
    backw_v[0:fields, 0:vel] = back_v[...]
    wide = backw_v[...]
    top = wide.astype(bf16).astype(f32)
    rest = wide - top
    turned = jnp.concatenate(
        [top, top, rest, rest, jnp.zeros((lanes - 4 * PAD, wide.shape[1]), f32)], axis=0
    ).T
    backs_v[...] = turned[0:vel].astype(bf16)
    wait_halo(0)
    bent = laplace(0, moments)
    target = [
        active * (mixed[c] - gain[c] * bent[c]) + inlet * moments[c] for c in range(fields)
    ]

    def omega(k):
        return 1.0 / (1.0 + 0.8 * math.cos(math.pi * (2 * k + 1) / (2 * ITERS)))

    def residual(k, w, coupled):
        bent = laplace(k, w)
        return [
            target[c] - (w[c] + active * diffusivity[c] * bent[c] - fluid * coupled[c])
            for c in range(fields)
        ]

    correction = [omega(0) * target[c] * inverse[c] for c in range(fields)]
    resid = target
    for k in range(1, ITERS):
        start_halo(k, correction)
        keep_squares(k - 1, resid)
        coupled = mix(coupling, correction)
        wait_halo(k)
        resid = residual(k, correction, coupled)
        correction = [
            correction[c] + omega(k) * resid[c] * inverse[c] for c in range(fields)
        ]
    start_halo(ITERS, correction)
    for c in range(fields):
        planes_v[me, tile(c), :] = correction[c]

    def gather(source, peer):
        return remote(
            planes_v.at[source, used], planes_v.at[source, used], ag_s.at[peer], ag_r.at[source],
            at(cx, cyz, peer),
        )

    for owner in order[:-1]:
        gather(me, owner).start()
    keep_squares(ITERS - 1, resid)
    coupled = mix(coupling, correction)

    size = vel // CHUNKS
    stores = []

    def finish(step):
        owner = order[step]
        if step < last:
            gather(owner, owner).wait_recv()
        columns = jnp.concatenate(
            [planes_v[owner, pl.ds(y, PAD, stride=rows), :] for y in range(rows)], axis=1
        )
        top, rest = halves(columns)
        stacked = jnp.concatenate(
            [top, rest, top, rest, jnp.zeros((lanes - 4 * PAD, rows * lanes), bf16)], axis=0
        )
        for chunk in range(CHUNKS):
            span = pl.ds(chunk * size, size)
            flat = delta_v.at[chunk].reshape(size * rows, lanes)
            for y in range(0, rows, 2):
                delta = jnp.dot(
                    backs_v[span, :], stacked[:, y * lanes:(y + 2) * lanes],
                    preferred_element_type=f32,
                )
                for i in range(2):
                    flat[pl.ds(y + i, size, stride=rows), :] = delta[:, i * lanes:(i + 1) * lanes]
            out_v[step, span] = (dist_v[step, span] + delta_v[chunk]).astype(bf16)
        copy = pltpu.make_async_copy(out_v.at[step], out.at[:, plane_of(owner)], out_sem.at[step])
        copy.start()
        stores.append(copy)

    finish(last)
    wait_halo(ITERS)
    keep_squares(ITERS, residual(ITERS, correction, coupled))
    mine = cx * nv + me
    first[mine] = lax.dot_general(
        jnp.ones((rows, lanes), f32), sq[...], (((1,), (1,)), ((), ())),
        precision=lax.Precision.HIGHEST, preferred_element_type=f32,
    )

    def sum_first(slot, index, c, v):
        return remote(first.at[slot], first.at[slot], a1_s.at[index], a1_r.at[slot], at(c, cyz, v))

    def sum_second(slot, index, y):
        return remote(second.at[slot], second.at[slot], a2_s.at[index], a2_r.at[slot], at(cx, y, me))

    for index, (dx, dv) in enumerate(group):
        sum_first(mine, index, (cx + dx) % ncx, (me + dv) % nv).start()
    finish(last - 1)
    for index, (dx, dv) in enumerate(group):
        c, v = (cx + dx) % ncx, (me + dv) % nv
        sum_first(c * nv + v, index, c, v).wait_recv()
    total = first[0]
    for i in range(1, ncx * nv):
        total = total + first[i]
    second[cyz] = total
    for dy in range(1, ncyz):
        sum_second(cyz, dy, (cyz + dy) % ncyz).start()
    for step in range(last - 2, -1, -1):
        finish(step)
    for dy in range(1, ncyz):
        y = (cyz + dy) % ncyz
        sum_second(y, dy, y).wait_recv()
    total = second[0]
    for i in range(1, ncyz):
        total = total + second[i]
    value = jnp.sqrt(total / (ncx * nv * rows * ncyz * lanes) + 1e-06)
    for k in range(ITERS + 1):
        shifted = value if k == 0 else pltpu.roll(value, lanes - k * fields, 1)
        norms[pl.ds(k, 1), :] = shifted[0:1, 0:fields]

    for owner in order[:-1]:
        scatter(owner, me).wait_send()
        gather(me, owner).wait_send()
    for k in range(ITERS + 1):
        for d in range(4):

            @pl.when(has[d])
            def _():
                halo(k, d).wait_send()

    for index, (dx, dv) in enumerate(group):
        sum_first(mine, index, (cx + dx) % ncx, (me + dv) % nv).wait_send()
    for dy in range(1, ncyz):
        sum_second(cyz, dy, (cyz + dy) % ncyz).wait_send()
    for copy in stores:
        copy.wait()


def local(mesh_shape, *args):
    dist, cell_type, basis = args[:3]
    ncx, ncyz, nv = mesh_shape
    vel, planes, rows, lanes = dist.shape
    fields = basis.shape[0]
    assert planes == nv and nv % 2 == 0 and vel % (CHUNKS * 16) == 0
    sizes = (ncx, ncyz, nv, fields, vel, rows, lanes)
    anywhere = pl.BlockSpec(memory_space=pl.ANY)
    held = pl.BlockSpec(memory_space=pltpu.HBM)
    rounds = ITERS + 1
    dma = pltpu.SemaphoreType.DMA
    deep = fields * rows
    return pl.pallas_call(
        functools.partial(kernel, sizes),
        out_shape=(
            jax.ShapeDtypeStruct(dist.shape, bf16),
            jax.ShapeDtypeStruct((rounds, fields), f32),
        ),
        in_specs=[held] * 8,
        out_specs=(anywhere, pl.BlockSpec(memory_space=pltpu.VMEM)),
        scratch_shapes=[
            pltpu.SMEM((fields, fields), f32),
            pltpu.SMEM((fields, fields), f32),
            pltpu.SMEM((fields,), f32),
            pltpu.SMEM((fields,), f32),
            pltpu.VMEM((nv, vel, rows, lanes), f32),
            pltpu.VMEM((nv, vel, rows, lanes), bf16),
            pltpu.VMEM((CHUNKS, vel // CHUNKS, rows, lanes), f32),
            pltpu.VMEM(cell_type.shape, jnp.int32),
            pltpu.VMEM((fields, vel), f32),
            pltpu.VMEM((PAD, vel), f32),
            pltpu.VMEM((fields, vel), f32),
            pltpu.VMEM((PAD, -(-vel // lanes) * lanes), f32),
            pltpu.VMEM((vel, lanes), bf16),
            pltpu.VMEM((nv, PAD * rows, lanes), f32),
            pltpu.VMEM((nv, deep, lanes), f32),
            pltpu.VMEM((rounds, deep, lanes), f32),
            pltpu.VMEM((rounds, 2, deep, lanes), f32),
            pltpu.VMEM((rounds, 2, fields, lanes), f32),
            pltpu.VMEM((rounds, 2, fields, lanes), f32),
            pltpu.VMEM((nv, PAD * rows, lanes), f32),
            pltpu.VMEM((lanes, lanes), f32),
            pltpu.VMEM((ncx * nv, rows, lanes), f32),
            pltpu.VMEM((ncyz, rows, lanes), f32),
            dma((nv,)), dma((7,)), dma((nv,)), dma((nv,)),
            dma((rounds, 4)), dma((rounds, 4)), dma((nv,)), dma((nv,)),
            dma((ncx * nv,)), dma((ncx * nv,)), dma((ncyz,)), dma((ncyz,)), dma((nv,)),
        ],
        compiler_params=pltpu.CompilerParams(
            collective_id=0, has_side_effects=True, vmem_limit_bytes=67043328
        ),
    )(*args[:3], args[3].T, *args[4:])


def solution(mesh):
    placed = (
        P("vert", "cx", "cyz", None),
        P("cx", "cyz", None),
        P(None, "vert"),
        P("vert", None),
        P(),
        P(),
        P(),
        P(),
    )
    shape = tuple(mesh.shape[name] for name in ("cx", "cyz", "vert"))
    return jax.shard_map(
        functools.partial(local, shape),
        mesh=mesh,
        in_specs=placed,
        out_specs=(P("vert", "cx", "cyz", None), P()),
        check_vma=False,
    )
```

```python
import functools
import math

import jax
import jax.numpy as jnp
from jax import lax
from jax.experimental import pallas as pl
from jax.experimental.pallas import tpu as pltpu
from jax.sharding import PartitionSpec as P

ITERS = 4
PAD = 16
CHUNKS = 3
MESH = pl.DeviceIdType.MESH
f32 = jnp.float32
bf16 = jnp.bfloat16


def halves(x):
    high = x.astype(bf16)
    return high, (x - high.astype(f32)).astype(bf16)


def kernel(
    sizes, dist, cell_type, basis, backmap, source_hbm, coupling_hbm, diffusivity_hbm, gain_hbm,
    out, norms,
    source_map, coupling, diffusivity, gain, dist_v, delta_v, cells_v, basis_v, wide_v, back_v, backw_v, backs_v,
    part, arrived, field, xh, ystage, yh, planes_v, sq, first, second,
    dist_sem, small_sem, rs_s, rs_r, h_s, h_r, ag_s, ag_r, a1_s, a1_r, a2_s, a2_r,
):
    ncx, ncyz, nv, fields, vel, rows, lanes = sizes
    cx, cyz, me = lax.axis_index("cx"), lax.axis_index("cyz"), lax.axis_index("vert")

    def at(c, y, v):
        return {"cx": c, "cyz": y, "vert": v}

    odd = cx % 2

    def plane_of(v):
        return v + odd * (nv - 1 - 2 * v)

    chip, core = me // 2, me % 2
    order = []
    for da in list(range(1, nv // 2)) + [0]:
        for db in (0, 1) if da else (1, 0):
            order.append(2 * ((chip + da) % (nv // 2)) + (core + db) % 2)
    last = nv - 1

    loads = []
    for step, owner in enumerate(order):
        copy = pltpu.make_async_copy(
            dist.at[:, plane_of(owner)], dist_v.at[step], dist_sem.at[step]
        )
        copy.start()
        loads.append(copy)
        if step == 0:
            get_basis = pltpu.make_async_copy(basis, basis_v, small_sem.at[0])
            get_basis.start()
    get_back = pltpu.make_async_copy(backmap, back_v, small_sem.at[1])
    get_cells = pltpu.make_async_copy(cell_type, cells_v, small_sem.at[2])
    get_back.start()
    get_cells.start()
    scalars = [
        pltpu.make_async_copy(a, b, small_sem.at[3 + i])
        for i, (a, b) in enumerate((
            (source_hbm, source_map), (coupling_hbm, coupling),
            (diffusivity_hbm, diffusivity), (gain_hbm, gain),
        ))
    ]
    for copy in scalars:
        copy.start()

    group = [
        (dx, dv) for dx in range(ncx) for dv in range(nv) if (dx, dv) != (0, 0)
    ]
    barrier = pltpu.get_barrier_semaphore()
    for dx, dv in group:
        pl.semaphore_signal(
            barrier, inc=1, device_id=at((cx + dx) % ncx, cyz, (me + dv) % nv), device_id_type=MESH
        )
    for dy in range(1, ncyz):
        pl.semaphore_signal(
            barrier, inc=1, device_id=at(cx, (cyz + dy) % ncyz, me), device_id_type=MESH
        )

    spot = plane_of(me)
    low, high = spot == 0, spot == nv - 1
    side = 1 - 2 * odd
    left = at(jnp.where(low, cx - 1, cx), cyz, jnp.where(low, me, me - side))
    right = at(jnp.where(high, cx + 1, cx), cyz, jnp.where(high, me, me + side))
    prev, following = at(cx, cyz - 1, me), at(cx, cyz + 1, me)
    place = cx * nv + spot
    has = [place > 0, place < ncx * nv - 1, cyz > 0, cyz < ncyz - 1]
    to = [left, right, prev, following]

    sq[...] = jnp.zeros_like(sq)
    planes_v[...] = jnp.zeros_like(planes_v)
    wide_v[...] = jnp.zeros_like(wide_v)
    for direction in range(2):

        @pl.when(jnp.logical_not(has[direction]))
        def _():
            for k in range(ITERS + 1):
                xh[k, direction] = jnp.zeros((fields * rows, lanes), f32)

        @pl.when(jnp.logical_not(has[2 + direction]))
        def _():
            for k in range(ITERS + 1):
                yh[k, direction] = jnp.zeros((fields, lanes), f32)

    get_basis.wait()
    wide_v[0:fields, :] = basis_v[...]
    weights = jnp.concatenate(halves(wide_v[...]), axis=0)

    def remote(src, dst, send, recv, device):
        return pltpu.make_async_remote_copy(
            src_ref=src, dst_ref=dst, send_sem=send, recv_sem=recv,
            device_id=device, device_id_type=MESH,
        )

    used = pl.ds(0, fields * rows)

    def scatter(owner, source):
        return remote(
            part.at[owner, used], arrived.at[source], rs_s.at[owner], rs_r.at[source],
            at(cx, cyz, owner),
        )

    for step, owner in enumerate(order):
        loads[step].wait()
        flat = dist_v.at[step].reshape(vel * rows, lanes)
        for y in range(0, rows, 2):
            pair = jnp.concatenate(
                [flat[pl.ds(y + i, vel, stride=rows), :] for i in range(2)], axis=1
            )
            top, rest = halves(pair)
            both = jnp.dot(weights, top, preferred_element_type=f32) + jnp.dot(
                weights, rest, preferred_element_type=f32
            )
            both = both[0:PAD] + both[PAD:]
            for i in range(2):
                part[owner, pl.ds(y + i, PAD, stride=rows), :] = both[:, i * lanes:(i + 1) * lanes]
        if step == 0:
            pl.semaphore_wait(barrier, len(group) + ncyz - 1)
        if step < last:
            scatter(owner, me).start()

    get_cells.wait()
    for copy in scalars:
        copy.wait()
    kinds = cells_v[spot]
    fluid = jnp.where(kinds == 0, 1.0, 0.0).astype(f32)
    inlet = jnp.where(kinds == 2, 1.0, 0.0).astype(f32)
    outlet = jnp.where(kinds == 3, 1.0, 0.0).astype(f32)
    active = fluid + outlet
    row = lax.broadcasted_iota(jnp.int32, (rows, lanes), 0)
    lane = lax.broadcasted_iota(jnp.int32, (rows, lanes), 1)

    def tile(c):
        return pl.ds(c * rows, rows)

    def mix(matrix, w):
        mixed = []
        for c in range(fields):
            total = matrix[c, 0] * w[0]
            for j in range(1, fields):
                total = total + matrix[c, j] * w[j]
            mixed.append(total)
        return mixed

    def halo(k, d):
        if d < 2:
            return remote(field.at[k], xh.at[k, 1 - d], h_s.at[k, d], h_r.at[k, 1 - d], to[d])
        return remote(
            ystage.at[k, d - 2], yh.at[k, 3 - d], h_s.at[k, d], h_r.at[k, 5 - d], to[d]
        )

    def landed(k, d):
        if d < 2:
            return remote(field.at[k], xh.at[k, d], h_s.at[k, d], h_r.at[k, d], to[d])
        return remote(ystage.at[k, d - 2], yh.at[k, d - 2], h_s.at[k, d], h_r.at[k, d], to[d])

    def start_halo(k, w):
        for c in range(fields):
            field[k, tile(c), :] = w[c]
            ystage[k, 0, pl.ds(c, 1), :] = w[c][0:1]
            ystage[k, 1, pl.ds(c, 1), :] = w[c][rows - 1:rows]
        for d in range(4):

            @pl.when(has[d])
            def _():
                halo(k, d).start()

    def wait_halo(k):
        for d in range(4):

            @pl.when(has[d])
            def _():
                landed(k, d).wait_recv()

    def laplace(k, w):
        result = []
        for c in range(fields):
            x = w[c]
            near = xh[k, 0, tile(c), :] + xh[k, 1, tile(c), :]
            above = jnp.broadcast_to(yh[k, 0, pl.ds(c, 1), :], (rows, lanes))
            below = jnp.broadcast_to(yh[k, 1, pl.ds(c, 1), :], (rows, lanes))
            near = near + jnp.where(row == 0, above, pltpu.roll(x, 1, 0))
            near = near + jnp.where(row == rows - 1, below, pltpu.roll(x, rows - 1, 0))
            near = near + jnp.where(lane == 0, 0.0, pltpu.roll(x, 1, 1))
            near = near + jnp.where(lane == lanes - 1, 0.0, pltpu.roll(x, lanes - 1, 1))
            result.append(6.0 * x - near)
        return result

    def keep_squares(k, r):
        for c in range(fields):
            sq[pl.ds(k * fields + c, 1), :] = jnp.sum(r[c] * r[c], axis=0, keepdims=True)

    for owner in order[:-1]:
        scatter(owner, owner).wait_recv()
    moments = []
    for c in range(fields):
        total = part[me, tile(c), :]
        for owner in order[:-1]:
            total = total + arrived[owner, tile(c), :]
        moments.append(total)

    start_halo(0, moments)
    mixed = mix(source_map, moments)
    inverse = [
        1.0 / (1.0 + 6.0 * active * diffusivity[c] - fluid * coupling[c, c])
        for c in range(fields)
    ]
    get_back.wait()
    backw_v[...] = jnp.zeros_like(backw_v)
    backw_v[0:fields, 0:vel] = back_v[...]
    wide = backw_v[...]
    top = wide.astype(bf16).astype(f32)
    rest = wide - top
    turned = jnp.concatenate(
        [top, top, rest, rest, jnp.zeros((lanes - 4 * PAD, wide.shape[1]), f32)], axis=0
    ).T
    backs_v[...] = turned[0:vel].astype(bf16)
    wait_halo(0)
    bent = laplace(0, moments)
    target = [
        active * (mixed[c] - gain[c] * bent[c]) + inlet * moments[c] for c in range(fields)
    ]

    def omega(k):
        return 1.0 / (1.0 + 0.8 * math.cos(math.pi * (2 * k + 1) / (2 * ITERS)))

    def residual(k, w, coupled):
        bent = laplace(k, w)
        return [
            target[c] - (w[c] + active * diffusivity[c] * bent[c] - fluid * coupled[c])
            for c in range(fields)
        ]

    correction = [omega(0) * target[c] * inverse[c] for c in range(fields)]
    resid = target
    for k in range(1, ITERS):
        start_halo(k, correction)
        keep_squares(k - 1, resid)
        coupled = mix(coupling, correction)
        wait_halo(k)
        resid = residual(k, correction, coupled)
        correction = [
            correction[c] + omega(k) * resid[c] * inverse[c] for c in range(fields)
        ]
    start_halo(ITERS, correction)
    for c in range(fields):
        planes_v[me, tile(c), :] = correction[c]

    def gather(source, peer):
        return remote(
            planes_v.at[source, used], planes_v.at[source, used], ag_s.at[peer], ag_r.at[source],
            at(cx, cyz, peer),
        )

    for owner in order[:-1]:
        gather(me, owner).start()
    keep_squares(ITERS - 1, resid)
    coupled = mix(coupling, correction)

    size = vel // CHUNKS

    def finish(step):
        owner = order[step]
        if step < last:
            gather(owner, owner).wait_recv()
        columns = jnp.concatenate(
            [planes_v[owner, pl.ds(y, PAD, stride=rows), :] for y in range(rows)], axis=1
        )
        top, rest = halves(columns)
        stacked = jnp.concatenate(
            [top, rest, top, rest, jnp.zeros((lanes - 4 * PAD, rows * lanes), bf16)], axis=0
        )
        for chunk in range(CHUNKS):
            span = pl.ds(chunk * size, size)
            flat = delta_v.at[chunk].reshape(size * rows, lanes)
            for y in range(0, rows, 2):
                delta = jnp.dot(
                    backs_v[span, :], stacked[:, y * lanes:(y + 2) * lanes],
                    preferred_element_type=f32,
                )
                for i in range(2):
                    flat[pl.ds(y + i, size, stride=rows), :] = delta[:, i * lanes:(i + 1) * lanes]
            out[span, plane_of(owner)] = (dist_v[step, span] + delta_v[chunk]).astype(bf16)

    finish(last)
    wait_halo(ITERS)
    keep_squares(ITERS, residual(ITERS, correction, coupled))
    mine = cx * nv + me
    first[mine] = lax.dot_general(
        jnp.ones((rows, lanes), f32), sq[...], (((1,), (1,)), ((), ())),
        precision=lax.Precision.HIGHEST, preferred_element_type=f32,
    )

    def sum_first(slot, index, c, v):
        return remote(first.at[slot], first.at[slot], a1_s.at[index], a1_r.at[slot], at(c, cyz, v))

    def sum_second(slot, index, y):
        return remote(second.at[slot], second.at[slot], a2_s.at[index], a2_r.at[slot], at(cx, y, me))

    for index, (dx, dv) in enumerate(group):
        sum_first(mine, index, (cx + dx) % ncx, (me + dv) % nv).start()
    finish(last - 1)
    for index, (dx, dv) in enumerate(group):
        c, v = (cx + dx) % ncx, (me + dv) % nv
        sum_first(c * nv + v, index, c, v).wait_recv()
    total = first[0]
    for i in range(1, ncx * nv):
        total = total + first[i]
    second[cyz] = total
    for dy in range(1, ncyz):
        sum_second(cyz, dy, (cyz + dy) % ncyz).start()
    for step in range(last - 2, -1, -1):
        finish(step)
    for dy in range(1, ncyz):
        y = (cyz + dy) % ncyz
        sum_second(y, dy, y).wait_recv()
    total = second[0]
    for i in range(1, ncyz):
        total = total + second[i]
    value = jnp.sqrt(total / (ncx * nv * rows * ncyz * lanes) + 1e-06)
    for k in range(ITERS + 1):
        shifted = value if k == 0 else pltpu.roll(value, lanes - k * fields, 1)
        norms[pl.ds(k, 1), :] = shifted[0:1, 0:fields]

    for owner in order[:-1]:
        scatter(owner, me).wait_send()
        gather(me, owner).wait_send()
    for k in range(ITERS + 1):
        for d in range(4):

            @pl.when(has[d])
            def _():
                halo(k, d).wait_send()

    for index, (dx, dv) in enumerate(group):
        sum_first(mine, index, (cx + dx) % ncx, (me + dv) % nv).wait_send()
    for dy in range(1, ncyz):
        sum_second(cyz, dy, (cyz + dy) % ncyz).wait_send()


def local(mesh_shape, *args):
    dist, cell_type, basis = args[:3]
    ncx, ncyz, nv = mesh_shape
    vel, planes, rows, lanes = dist.shape
    fields = basis.shape[0]
    assert planes == nv and nv % 2 == 0 and vel % (CHUNKS * 16) == 0
    sizes = (ncx, ncyz, nv, fields, vel, rows, lanes)
    held = pl.BlockSpec(memory_space=pltpu.HBM)
    rounds = ITERS + 1
    dma = pltpu.SemaphoreType.DMA
    deep = fields * rows
    return pl.pallas_call(
        functools.partial(kernel, sizes),
        out_shape=(
            pltpu.VMEM(dist.shape, bf16),
            jax.ShapeDtypeStruct((rounds, fields), f32),
        ),
        in_specs=[held] * 8,
        out_specs=(pl.BlockSpec(memory_space=pltpu.VMEM),) * 2,
        scratch_shapes=[
            pltpu.SMEM((fields, fields), f32),
            pltpu.SMEM((fields, fields), f32),
            pltpu.SMEM((fields,), f32),
            pltpu.SMEM((fields,), f32),
            pltpu.VMEM((nv, vel, rows, lanes), f32),
            pltpu.VMEM((CHUNKS, vel // CHUNKS, rows, lanes), f32),
            pltpu.VMEM(cell_type.shape, jnp.int32),
            pltpu.VMEM((fields, vel), f32),
            pltpu.VMEM((PAD, vel), f32),
            pltpu.VMEM((fields, vel), f32),
            pltpu.VMEM((PAD, -(-vel // lanes) * lanes), f32),
            pltpu.VMEM((vel, lanes), bf16),
            pltpu.VMEM((nv, PAD * rows, lanes), f32),
            pltpu.VMEM((nv, deep, lanes), f32),
            pltpu.VMEM((rounds, deep, lanes), f32),
            pltpu.VMEM((rounds, 2, deep, lanes), f32),
            pltpu.VMEM((rounds, 2, fields, lanes), f32),
            pltpu.VMEM((rounds, 2, fields, lanes), f32),
            pltpu.VMEM((nv, PAD * rows, lanes), f32),
            pltpu.VMEM((lanes, lanes), f32),
            pltpu.VMEM((ncx * nv, rows, lanes), f32),
            pltpu.VMEM((ncyz, rows, lanes), f32),
            dma((nv,)), dma((7,)), dma((nv,)), dma((nv,)),
            dma((rounds, 4)), dma((rounds, 4)), dma((nv,)), dma((nv,)),
            dma((ncx * nv,)), dma((ncx * nv,)), dma((ncyz,)), dma((ncyz,)),
        ],
        compiler_params=pltpu.CompilerParams(
            collective_id=0, has_side_effects=True, vmem_limit_bytes=58 * 10**6
        ),
    )(*args[:3], args[3].T, *args[4:])


def solution(mesh):
    placed = (
        P("vert", "cx", "cyz", None),
        P("cx", "cyz", None),
        P(None, "vert"),
        P("vert", None),
        P(),
        P(),
        P(),
        P(),
    )
    shape = tuple(mesh.shape[name] for name in ("cx", "cyz", "vert"))
    return jax.shard_map(
        functools.partial(local, shape),
        mesh=mesh,
        in_specs=placed,
        out_specs=(P("vert", "cx", "cyz", None), P()),
        check_vma=False,
    )
```
